256 devices in a mesh: wide: 32 (over x, z_hi, core), narrow: 8 (over y, z_lo).
Axes of the slice: x: 4, y: 4, z: 8 (z_hi: 4, z_lo: 2; z = z_hi * 2 + z_lo), core: 2. Of those that a mesh axis runs over, the one named last changes fastest.
Arguments:
- initial: float32 [32, 8, 128, 2048], P('wide', 'narrow'), may hold values from -6 to 6
- block_values: bfloat16 [16, 12, 128, 128], replicated, may hold values from -0.0546875 to 0.0546875
- block_index: int32 [16, 12], replicated, may hold values from 0 to 15, as said below
- bond_sites: int32 [12, 2], replicated, may hold values from 0 to 6, as said below
- bond_coupling: float32 [12], replicated, may hold values from -0.25 to 0.25
- pin_sites: int32 [8], replicated, may hold values from 0 to 6
- pin_partner: int32 [8], replicated, may hold values from 0 to 13
- pinned_spins: int32 [14], replicated, may hold values from 0 to 1
- pin_coupling: float32 [8], replicated, may hold values from -0.2 to 0.2
- cross_sites: int32 [4], replicated, may hold values from 0 to 6
- cross_coupling: float32 [4], replicated, may hold values from 0.2 to 0.4
Outputs:
- previous_vector: float32 [32, 8, 128, 2048], P('wide', 'narrow')
- chebyshev_vector: float32 [32, 8, 128, 2048], P('wide', 'narrow')
The draws below stay inside these ranges and needn't reach their ends.
Inputs may be any that keep to these rules, and one draw needn't show every extreme that they name: `block_index`: each row names 12 different block columns. `bond_sites`: the two spins of a bond differ.
All inputs are finite; a program needn't handle non-finite values.
Results may differ from the reference program's by a relative error of at most 0.0031.
Values may be sent and summed in bfloat16 or wider, within the bound.
A program may use at most 128 MiB of HBM per device.

```python
import jax
import jax.numpy as jnp
from jax import lax

BLOCK = 128
KBLOCKS = 12
BROWS = 16
LOWDIM = 2048
CBITS = 7
COLUMNS = 128
BONDS = 12
PBONDS = 8
PINNED = 14
CROSS = 4
STEPS = 4
WSLABS = 32
NSLABS = 8


def draw_block_index(key, part):
    row_keys = jax.random.split(jax.random.fold_in(key, 11), BROWS)
    orders = jax.vmap(lambda one_key: jax.random.permutation(one_key, BROWS))(row_keys)
    return orders[:, :KBLOCKS].astype(jnp.int32)


def draw_bond_sites(key, part):
    first_key, second_key = jax.random.split(jax.random.fold_in(key, 23))
    site_one = jax.random.randint(first_key, (BONDS,), 0, CBITS)
    offset = jax.random.randint(second_key, (BONDS,), 1, CBITS)
    site_two = (site_one + offset) % CBITS
    return jnp.stack([site_one, site_two], axis=1).astype(jnp.int32)


def plant(result, own_key, low, largest):
    dims = result.shape
    index_at = [jax.random.randint(jax.random.fold_in(own_key, axis), (), 0, dims[axis]) for axis in range(len(dims))]
    result = result.at[tuple(index_at)].set(low)
    longest = dims.index(max(dims))
    index_at[longest] = (index_at[longest] + 1) % dims[longest]
    return result.at[tuple(index_at)].set(largest)


def levels(stream_key, shape, pieces, low, largest):
    level = 1.0
    for axis_at, shards_of in pieces:
        steps = jax.random.uniform(jax.random.fold_in(jax.random.fold_in(stream_key, 6), axis_at), (shards_of,), jnp.float32, low / len(pieces), largest / len(pieces))
        level = level * jnp.repeat(jnp.exp(steps), shape[axis_at] // shards_of).reshape((-1,) + (1,) * (len(shape) - 1 - axis_at))
    return level


def normal_values(own_key, extent, width, most, shards=(), held_as=jnp.bfloat16):
    drawn = jax.random.normal(own_key, extent, jnp.float32) * width
    if len(shards) > 0:
        drawn = levels(own_key, extent, shards, -0.22, 0.18) * drawn
    return jnp.clip(drawn, min=-most, max=most).astype(held_as)


def setup_inputs(seed: int = 0) -> dict:
    keys = jax.random.split(jax.random.key(seed), 12)
    return {
        "initial": normal_values(keys[0], (WSLABS, NSLABS, COLUMNS, LOWDIM), 1.0, 6.0, ((0, 32), (1, 8)), jnp.float32),
        "block_values": normal_values(keys[1], (BROWS, KBLOCKS, BLOCK, BLOCK), (8 * KBLOCKS * BLOCK) ** -0.5, 0.0546875),
        "block_index": draw_block_index(jax.random.fold_in(keys[11], 71), 0),
        "bond_sites": draw_bond_sites(jax.random.fold_in(keys[11], 71), 0),
        "bond_coupling": jnp.clip(jax.random.uniform(keys[4], (BONDS,), jnp.float32, -0.25, 0.25), -0.25, 0.25),
        "pin_sites": plant(jax.random.randint(keys[5], (PBONDS,), 0, CBITS), jax.random.fold_in(keys[5], 1), 0, CBITS - 1).astype(jnp.int32),
        "pin_partner": plant(jax.random.randint(keys[6], (PBONDS,), 0, PINNED), jax.random.fold_in(keys[6], 1), 0, PINNED - 1).astype(jnp.int32),
        "pinned_spins": plant(jax.random.randint(keys[7], (PINNED,), 0, 2), jax.random.fold_in(keys[7], 1), 0, 1).astype(jnp.int32),
        "pin_coupling": jnp.clip(jax.random.uniform(keys[8], (PBONDS,), jnp.float32, -0.2, 0.2), -0.2, 0.2),
        "cross_sites": plant(jax.random.randint(keys[9], (CROSS,), 0, CBITS), jax.random.fold_in(keys[9], 1), 0, CBITS - 1).astype(jnp.int32),
        "cross_coupling": jnp.clip(jax.random.uniform(keys[10], (CROSS,), jnp.float32, 0.2, 0.4), 0.2, 0.4),
    }


def bit_at(values, position):
    return jnp.bitwise_and(jnp.right_shift(values, position), 1)


def column_operator(bond_sites, bond_coupling, pin_sites, pin_partner, pinned_spins, pin_coupling):
    columns = jnp.arange(COLUMNS, dtype=jnp.int32)
    site_one = bit_at(columns[None, :], bond_sites[:, 0:1])
    site_two = bit_at(columns[None, :], bond_sites[:, 1:2])
    differ = (site_one != site_two).astype(jnp.float32)
    flip_bits = jnp.bitwise_xor(jnp.left_shift(jnp.int32(1), bond_sites[:, 0:1]), jnp.left_shift(jnp.int32(1), bond_sites[:, 1:2]))
    target = jnp.bitwise_xor(columns[None, :], flip_bits)
    hopping = (target[:, :, None] == columns[None, None, :]).astype(jnp.float32)
    hopping_part = jnp.sum((bond_coupling[:, None] * differ * 0.5)[:, :, None] * hopping, axis=0)
    diagonal = jnp.sum(bond_coupling[:, None] * (1.0 - 2.0 * differ) * 0.25, axis=0)
    chosen = pin_partner[:, None] == jnp.arange(PINNED, dtype=jnp.int32)[None, :]
    pinned = jnp.sum(jnp.where(chosen, pinned_spins[None, :], 0), axis=1).astype(jnp.int32)
    pin_bits = bit_at(columns[None, :], pin_sites[:, None])
    aligned = jnp.bitwise_xor(pin_bits, pinned[:, None]).astype(jnp.float32)
    pin_field = jnp.sum(pin_coupling[:, None] * (1.0 - 2.0 * aligned) * 0.25, axis=0)
    return hopping_part + jnp.diag(diagonal + pin_field)


def apply_whole(state, matrix, values_wide, block_index, cross_sites, cross_coupling):
    rounded = state.astype(jnp.bfloat16)
    flat = rounded.reshape(WSLABS * NSLABS, COLUMNS, BROWS, BLOCK)

    def one_slab(slab):
        blocks = jnp.take(slab, block_index, axis=1).astype(jnp.float32)
        return jnp.einsum("crkp,rkpq->crq", blocks, values_wide, precision=lax.Precision.HIGHEST)

    low_part = lax.map(one_slab, flat).reshape(state.shape)
    column_part = jnp.einsum("cd,wndl->wncl", matrix, state, precision=lax.Precision.HIGHEST)
    summed = low_part + column_part
    wide_log = WSLABS.bit_length() - 1
    narrow_log = NSLABS.bit_length() - 1
    columns = jnp.arange(COLUMNS, dtype=jnp.int32)
    for bond_slot, slab_axis, position, slab_count in ((0, 0, wide_log - 1, WSLABS), (1, 0, 0, WSLABS), (2, 1, narrow_log - 1, NSLABS), (3, 1, 0, NSLABS)):
        slab_ids = jnp.arange(slab_count, dtype=jnp.int32)
        own_bits = bit_at(slab_ids, position)
        partner_ids = jnp.bitwise_xor(slab_ids, 1 << position).astype(jnp.int32)
        partner = jnp.take(rounded, partner_ids, axis=slab_axis)
        cross_site = cross_sites[bond_slot]
        column_bit = bit_at(columns, cross_site)
        flipped_ids = jnp.bitwise_xor(columns, jnp.left_shift(jnp.int32(1), cross_site)).astype(jnp.int32)
        flipped = jnp.take(partner, flipped_ids, axis=2).astype(jnp.float32)
        if slab_axis == 0:
            own_shaped = own_bits.reshape((-1, 1, 1, 1))
        else:
            own_shaped = own_bits.reshape((1, -1, 1, 1))
        parity = jnp.bitwise_xor(own_shaped, column_bit.reshape((1, 1, -1, 1))).astype(jnp.float32)
        summed = summed + cross_coupling[bond_slot] * ((1.0 - 2.0 * parity) * 0.25 * state + parity * 0.5 * flipped)
    return summed


def reference(initial, block_values, block_index, bond_sites, bond_coupling, pin_sites, pin_partner, pinned_spins, pin_coupling, cross_sites, cross_coupling):
    matrix = column_operator(bond_sites, bond_coupling, pin_sites, pin_partner, pinned_spins, pin_coupling)
    values_wide = block_values.astype(jnp.float32)
    previous = initial
    current = apply_whole(previous, matrix, values_wide, block_index, cross_sites, cross_coupling)
    for repeat in range(STEPS - 1):
        following = 2.0 * apply_whole(current, matrix, values_wide, block_index, cross_sites, cross_coupling) - previous
        previous, current = current, following
    return previous, current
```

```python
import functools

import jax
import jax.numpy as jnp
from jax import lax
from jax.experimental import pallas as pl
from jax.experimental.pallas import tpu as pltpu
from jax.sharding import PartitionSpec as P

MESH = pl.DeviceIdType.MESH
STEPS = 4
CROSS = 4
CHUNK = 256


def bit_at(values, position):
    return jnp.bitwise_and(jnp.right_shift(values, position), 1)


def by_bond(bond, scalars):
    chosen = jnp.full(bond.shape, scalars[0])
    for k in range(1, CROSS):
        chosen = jnp.where(bond == k, scalars[k], chosen)
    return chosen


def packed_column(packed, site, bit):
    low = jnp.bitwise_and(packed, jnp.left_shift(1, site) - 1)
    high = jnp.left_shift(jnp.right_shift(packed, site), site + 1)
    return high | low | jnp.left_shift(bit, site)


def kernel(
    sizes,
    initial,
    block_values,
    block_index,
    bond_sites,
    bond_coupling,
    pin_sites,
    pin_partner,
    pinned_spins,
    pin_coupling,
    cross_sites,
    cross_coupling,
    previous_out,
    current_out,
    values,
    states,
    high,
    low,
    sent,
    received,
    mixer,
    picker,
    load_sem,
    value_sem,
    store_sem,
    send_sem,
    recv_sem,
):
    wide_log, narrow_log, columns, chunks, kept, bonds, pins = sizes
    half = columns // 2
    wide, narrow = lax.axis_index("wide"), lax.axis_index("narrow")
    own_bits = (
        bit_at(wide, wide_log - 1),
        bit_at(wide, 0),
        bit_at(narrow, narrow_log - 1),
        bit_at(narrow, 0),
    )

    def flipped(index, bit, position):
        return index + (1 - 2 * bit) * (1 << position)

    partners = (
        (flipped(wide, own_bits[0], wide_log - 1), narrow),
        (flipped(wide, own_bits[1], 0), narrow),
        (wide, flipped(narrow, own_bits[2], narrow_log - 1)),
        (wide, flipped(narrow, own_bits[3], 0)),
    )

    def load(j):
        return pltpu.make_async_copy(
            initial.at[0, 0, :, pl.ds(pl.multiple_of(j * CHUNK, CHUNK), CHUNK)],
            states.at[1, j],
            load_sem.at[j],
        )

    def load_values(j):
        return pltpu.make_async_copy(
            block_values.at[pl.ds(2 * j, 2)], values.at[pl.ds(2 * j, 2)], value_sem.at[j]
        )

    def exchange(step, j, k):
        rows = pl.ds(k * half, half)
        return pltpu.make_async_remote_copy(
            src_ref=sent.at[step, j, rows],
            dst_ref=received.at[step, j, rows],
            send_sem=send_sem.at[step, j, k],
            recv_sem=recv_sem.at[step, j, k],
            device_id=partners[k],
            device_id_type=MESH,
        )

    def store(out, slot, j):
        return pltpu.make_async_copy(
            states.at[slot, j],
            out.at[0, 0, :, pl.ds(pl.multiple_of(j * CHUNK, CHUNK), CHUNK)],
            store_sem.at[slot - STEPS, j],
        )

    def put(step, j, state):
        rounded = state.astype(jnp.bfloat16)
        packed = jnp.dot(picker[...], rounded, preferred_element_type=jnp.float32)
        sent[step, j] = packed.astype(jnp.bfloat16)
        rest = (state - rounded.astype(jnp.float32)).astype(jnp.bfloat16)
        for part in range(2):
            lanes = slice(part * 128, part * 128 + 128)
            high[step, 2 * j + part] = rounded[:, lanes]
            low[step, 2 * j + part] = rest[:, lanes]
        for k in range(CROSS):
            exchange(step, j, k).start()

    for j in range(chunks):
        load(j).start()
    for j in range(chunks):
        load_values(j).start()
    barrier = pltpu.get_barrier_semaphore()
    for partner in partners:
        pl.semaphore_signal(barrier, inc=1, device_id=partner, device_id_type=MESH)

    sites = [cross_sites[k] for k in range(CROSS)]
    row = lax.broadcasted_iota(jnp.int32, (CROSS * half, columns), 0)
    column = lax.broadcasted_iota(jnp.int32, (CROSS * half, columns), 1)
    bond = row // half
    wanted = packed_column(
        row % half, by_bond(bond, sites), 1 - by_bond(bond, own_bits)
    )
    picker[...] = jnp.where(wanted == column, 1.0, 0.0).astype(jnp.bfloat16)
    pl.semaphore_wait(barrier, CROSS)

    @pl.loop(0, chunks)
    def _(j):
        load(j).wait()
        put(0, j, states[1, j])

    states[0] = jnp.zeros(states.shape[1:], jnp.float32)

    row = lax.broadcasted_iota(jnp.int32, (columns, CROSS * half), 0)
    column = lax.broadcasted_iota(jnp.int32, (columns, CROSS * half), 1)
    bond = column // half
    arriving = packed_column(
        column % half, by_bond(bond, sites), 1 - by_bond(bond, own_bits)
    )
    strength = by_bond(bond, [cross_coupling[k] * 0.5 for k in range(CROSS)])
    crossing = jnp.where(arriving == row, strength, 0.0)
    crossing_high = crossing.astype(jnp.bfloat16)
    crossing_low = (crossing - crossing_high.astype(jnp.float32)).astype(jnp.bfloat16)

    row = lax.broadcasted_iota(jnp.int32, (columns, columns), 0)
    column = lax.broadcasted_iota(jnp.int32, (columns, columns), 1)
    hopping = jnp.zeros((columns, columns), jnp.float32)
    diagonal = jnp.zeros((columns, columns), jnp.float32)
    for b in range(bonds):
        one, two = bond_sites[b, 0], bond_sites[b, 1]
        differ = jnp.bitwise_xor(bit_at(row, one), bit_at(row, two)).astype(jnp.float32)
        target = jnp.bitwise_xor(row, jnp.left_shift(1, one) ^ jnp.left_shift(1, two))
        hopping += jnp.where(target == column, bond_coupling[b] * 0.5 * differ, 0.0)
        diagonal += bond_coupling[b] * 0.25 * (1.0 - 2.0 * differ)
    for p in range(pins):
        aligned = jnp.bitwise_xor(bit_at(row, pin_sites[p]), pinned_spins[pin_partner[p]])
        diagonal += pin_coupling[p] * 0.25 * (1.0 - 2.0 * aligned.astype(jnp.float32))
    for k in range(CROSS):
        parity = jnp.bitwise_xor(bit_at(row, sites[k]), own_bits[k])
        diagonal += cross_coupling[k] * 0.25 * (1.0 - 2.0 * parity.astype(jnp.float32))
    matrix = hopping + jnp.where(row == column, diagonal, 0.0)
    matrix_high = matrix.astype(jnp.bfloat16)
    matrix_low = (matrix - matrix_high.astype(jnp.float32)).astype(jnp.bfloat16)
    mixer[...] = jnp.concatenate(
        [crossing_high, crossing_low, matrix_high, matrix_high, matrix_low], axis=1
    )
    for j in range(chunks):
        load_values(j).wait()

    @pl.loop(0, STEPS)
    def _(step):
        scale = jnp.where(step == 0, 1.0, 2.0)

        @pl.loop(0, chunks)
        def _(j):
            parts = []
            for part in range(2):
                r = 2 * j + part
                gathered = jnp.concatenate(
                    [high[step, block_index[r, q]] for q in range(kept)], axis=1
                )
                blocks = values[r].reshape(kept * 128, 128)
                parts.append(jnp.dot(gathered, blocks, preferred_element_type=jnp.float32))
            total = jnp.concatenate(parts, axis=1)
            own_high = jnp.concatenate([high[step, 2 * j], high[step, 2 * j + 1]], axis=1)
            own_low = jnp.concatenate([low[step, 2 * j], low[step, 2 * j + 1]], axis=1)
            for k in range(CROSS):
                exchange(step, j, k).wait_recv()
            arrived = received[step, j]
            mixed = jnp.concatenate([arrived, arrived, own_high, own_low, own_high], axis=0)
            total += jnp.dot(mixer[...], mixed, preferred_element_type=jnp.float32)
            state = scale * total - states[step, j]
            states[step + 2, j] = state

            @pl.when(step < STEPS - 1)
            def _():
                put(step + 1, j, state)

            @pl.when(step == STEPS - 2)
            def _():
                store(previous_out, STEPS, j).start()

            @pl.when(step == STEPS - 1)
            def _():
                store(current_out, STEPS + 1, j).start()

    @pl.loop(0, STEPS)
    def _(step):
        @pl.loop(0, chunks)
        def _(j):
            for k in range(CROSS):
                exchange(step, j, k).wait_send()

    @pl.loop(0, chunks)
    def _(j):
        store(previous_out, STEPS, j).wait()
        store(current_out, STEPS + 1, j).wait()


def solution(mesh):
    wide_log = mesh.shape["wide"].bit_length() - 1
    narrow_log = mesh.shape["narrow"].bit_length() - 1

    def shards(initial, block_values, block_index, bond_sites, *rest):
        columns, width = initial.shape[2:]
        rows, kept = block_index.shape
        chunks = width // CHUNK
        sizes = (
            wide_log,
            narrow_log,
            columns,
            chunks,
            kept,
            bond_sites.shape[0],
            rest[1].shape[0],
        )
        whole = jax.ShapeDtypeStruct(initial.shape, jnp.float32)
        packed = (STEPS, chunks, CROSS * columns // 2, CHUNK)
        return pl.pallas_call(
            functools.partial(kernel, sizes),
            out_shape=(whole, whole),
            in_specs=[pl.BlockSpec(memory_space=pl.ANY)] * 2
            + [pl.BlockSpec(memory_space=pltpu.SMEM)] * 9,
            out_specs=(pl.BlockSpec(memory_space=pl.ANY),) * 2,
            scratch_shapes=[
                pltpu.VMEM(block_values.shape, jnp.bfloat16),
                pltpu.VMEM((STEPS + 2, chunks, columns, CHUNK), jnp.float32),
                pltpu.VMEM((STEPS, rows, columns, 128), jnp.bfloat16),
                pltpu.VMEM((STEPS, rows, columns, 128), jnp.bfloat16),
                pltpu.VMEM(packed, jnp.bfloat16),
                pltpu.VMEM(packed, jnp.bfloat16),
                pltpu.VMEM((columns, 2 * CROSS * columns // 2 + 3 * columns), jnp.bfloat16),
                pltpu.VMEM((CROSS * columns // 2, columns), jnp.bfloat16),
                pltpu.SemaphoreType.DMA((chunks,)),
                pltpu.SemaphoreType.DMA((chunks,)),
                pltpu.SemaphoreType.DMA((2, chunks)),
                pltpu.SemaphoreType.DMA((STEPS, chunks, CROSS)),
                pltpu.SemaphoreType.DMA((STEPS, chunks, CROSS)),
            ],
            compiler_params=pltpu.CompilerParams(
                collective_id=0, has_side_effects=True, vmem_limit_bytes=48 * 1024 * 1024
            ),
        )(initial, block_values, block_index, bond_sites, *rest)

    slab = P("wide", "narrow", None, None)
    return jax.shard_map(
        shards,
        mesh=mesh,
        in_specs=(slab,) + (P(),) * 10,
        out_specs=(slab, slab),
        check_vma=False,
    )
```

```python
import functools

import jax
import jax.numpy as jnp
from jax import lax
from jax.experimental import pallas as pl
from jax.experimental.pallas import tpu as pltpu
from jax.sharding import PartitionSpec as P

MESH = pl.DeviceIdType.MESH
STEPS = 4
CROSS = 4
CHUNK = 256


def bit_at(values, position):
    return jnp.bitwise_and(jnp.right_shift(values, position), 1)


def squeezed(columns, site):
    kept = jnp.bitwise_and(columns, jnp.left_shift(1, site) - 1)
    return kept | jnp.left_shift(jnp.right_shift(columns, site + 1), site)


def spread(packed, site, bit):
    kept = jnp.bitwise_and(packed, jnp.left_shift(1, site) - 1)
    high = jnp.left_shift(jnp.right_shift(packed, site), site + 1)
    return high | kept | jnp.left_shift(bit, site)


def lanes(count):
    return lax.broadcasted_iota(jnp.int32, (1, count), 1)


def rows_of(count, width):
    return lax.broadcasted_iota(jnp.int32, (count, width), 0)


def split(values):
    scaled = values * 65537.0
    high = scaled - (scaled - values)
    return high, values - high


def kernel(
    sizes,
    initial,
    block_values,
    *refs,
):
    smalls, (previous_out, current_out), refs = refs[:9], refs[9:11], refs[11:]
    (
        block_index,
        bond_sites,
        bond_coupling,
        pin_sites,
        pin_partner,
        pinned_spins,
        pin_coupling,
        cross_sites,
        cross_coupling,
    ) = refs[:9]
    (
        values,
        dense,
        states,
        high,
        low,
        ahead,
        sent,
        received,
        mixer,
        crosser,
        picker,
        small_sem,
        load_sem,
        value_sem,
        send_sem,
        recv_sem,
    ) = refs[9:]
    wide_log, narrow_log, columns, chunks, kept, bonds, pins = sizes
    rows = 2 * chunks
    half = columns // 2
    wide, narrow = lax.axis_index("wide"), lax.axis_index("narrow")
    own_bits = (
        bit_at(wide, wide_log - 1),
        bit_at(wide, 0),
        bit_at(narrow, narrow_log - 1),
        bit_at(narrow, 0),
    )

    def flipped(index, bit, position):
        return index + (1 - 2 * bit) * (1 << position)

    partners = (
        (flipped(wide, own_bits[0], wide_log - 1), narrow),
        (flipped(wide, own_bits[1], 0), narrow),
        (wide, flipped(narrow, own_bits[2], narrow_log - 1)),
        (wide, flipped(narrow, own_bits[3], 0)),
    )
    barrier = pltpu.get_barrier_semaphore()
    for partner in partners:
        pl.semaphore_signal(barrier, inc=1, device_id=partner, device_id_type=MESH)

    def load_small(i):
        return pltpu.make_async_copy(smalls[i], refs[i], small_sem.at[i])

    def load(j):
        return pltpu.make_async_copy(
            initial.at[0, 0, :, pl.ds(pl.multiple_of(j * CHUNK, CHUNK), CHUNK)],
            states.at[1, j],
            load_sem.at[j],
        )

    def load_values(j):
        pair = pl.ds(2 * j, 2)
        return pltpu.make_async_copy(
            block_values.at[pair], values.at[pair, pl.ds(0, kept)], value_sem.at[j]
        )

    def exchange(step, j, k):
        return pltpu.make_async_remote_copy(
            src_ref=sent.at[step, j, k],
            dst_ref=received.at[step, j, k],
            send_sem=send_sem.at[step, j, k],
            recv_sem=recv_sem.at[step, j, k],
            device_id=partners[k],
            device_id_type=MESH,
        )

    def store(out, j, state):
        out[0, 0, :, pl.ds(pl.multiple_of(j * CHUNK, CHUNK), CHUNK)] = state

    def keep(step, j, state):
        rounded = state.astype(jnp.bfloat16)
        rest = (state - rounded.astype(jnp.float32)).astype(jnp.bfloat16)
        for pair in range(CROSS // 2):
            wanted = picker[pair * columns : pair * columns + columns, :]
            packed = jnp.dot(wanted, rounded, preferred_element_type=jnp.float32)
            packed = packed.astype(jnp.bfloat16)
            for k in range(2):
                for h in range(2):
                    sent[step, j, 2 * pair + k, h] = packed[
                        k * half : k * half + half, h * 128 : h * 128 + 128
                    ]
        for h in range(2):
            high[step, 2 * j + h] = rounded[:, h * 128 : h * 128 + 128]
            low[step, 2 * j + h] = rest[:, h * 128 : h * 128 + 128]

    def send(step, j):
        for k in range(CROSS):
            exchange(step, j, k).start()

    for i in range(9):
        load_small(i).start()
    for j in range(chunks):
        load(j).start()
    for j in range(chunks):
        load_values(j).start()
    for i in range(9):
        load_small(i).wait()

    sites = [cross_sites[k] for k in range(CROSS)]
    column = lanes(columns)
    for k in range(CROSS):
        places = jnp.where(
            bit_at(column, sites[k]) == own_bits[k], -1, squeezed(column, sites[k])
        )
        chosen = rows_of(half, columns) == places
        picker[k * half : k * half + half, :] = jnp.where(chosen, 1.0, 0.0).astype(jnp.bfloat16)

    @pl.loop(0, chunks)
    def _(j):
        load(j).wait()
        keep(0, j, states[1, j])

    pl.semaphore_wait(barrier, CROSS)

    @pl.loop(0, chunks)
    def _(j):
        send(0, j)

    crossing = [[], []]
    for pair in range(CROSS // 2):
        upper = lanes(columns) >= half
        one, two = 2 * pair, 2 * pair + 1

        def either(first, second):
            return jnp.where(upper, second, first)

        arriving = spread(
            jnp.bitwise_and(lanes(columns), half - 1),
            either(sites[one], sites[two]),
            either(1 - own_bits[one], 1 - own_bits[two]),
        )
        met = rows_of(columns, columns) == arriving
        strengths = zip(split(cross_coupling[one] * 0.5), split(cross_coupling[two] * 0.5))
        for part, (first, second) in zip(crossing, strengths):
            part.append(jnp.where(met, either(first, second), 0.0).astype(jnp.bfloat16))
    for i in range(2):
        crosser[i] = jnp.concatenate(crossing[i], axis=1)

    row = rows_of(columns, columns)
    hopping = jnp.zeros((columns, columns), jnp.float32)
    diagonal = jnp.zeros((1, columns), jnp.float32)
    for b in range(bonds):
        one, two = bond_sites[0, b], bond_sites[1, b]
        differ = jnp.bitwise_xor(bit_at(column, one), bit_at(column, two)).astype(jnp.float32)
        source = jnp.bitwise_xor(column, jnp.left_shift(1, one) ^ jnp.left_shift(1, two))
        hopping += jnp.where(row == source, bond_coupling[b] * 0.5 * differ, 0.0)
        diagonal += bond_coupling[b] * 0.25 * (1.0 - 2.0 * differ)
    for p in range(pins):
        aligned = jnp.bitwise_xor(bit_at(column, pin_sites[p]), pinned_spins[pin_partner[p]])
        diagonal += pin_coupling[p] * 0.25 * (1.0 - 2.0 * aligned.astype(jnp.float32))
    for k in range(CROSS):
        parity = jnp.bitwise_xor(bit_at(column, sites[k]), own_bits[k])
        diagonal += cross_coupling[k] * 0.25 * (1.0 - 2.0 * parity.astype(jnp.float32))
    matrix = [
        part.astype(jnp.bfloat16) for part in split(hopping + jnp.where(row == column, diagonal, 0.0))
    ]
    mixer[...] = jnp.concatenate([matrix[0], matrix[0], matrix[1]], axis=1)
    states[0] = jnp.zeros(states.shape[1:], jnp.float32)
    values[:, kept] = jnp.zeros((rows, 128, 128), jnp.bfloat16)

    for j in range(chunks):
        load_values(j).wait()

    @pl.loop(0, chunks)
    def _(j):
        for part in range(2):
            r = 2 * j + part
            empty = sum(kept << 4 * i for i in range(8))
            places = [jnp.int32(empty - (1 << 32) if empty >> 31 else empty)] * 2
            for q in range(kept):
                wanted = block_index[r, q]
                shift = 4 * jnp.bitwise_and(wanted, 7)
                moved = jnp.left_shift(jnp.int32(q - kept), shift)
                upper = wanted >= 8
                places = [
                    places[0] + jnp.where(upper, 0, moved),
                    places[1] + jnp.where(upper, moved, 0),
                ]
            for m in range(rows):
                q = jnp.bitwise_and(jnp.right_shift(places[m // 8], 4 * (m % 8)), 15)
                dense[j, part, m] = values[r, jnp.minimum(q, kept)]

    def own_product(step, j):
        left = jnp.concatenate([high[step, m] for m in range(rows)] + [mixer[...]], axis=1)
        right = []
        for h in range(2):
            own_high, own_low = high[step, 2 * j + h], low[step, 2 * j + h]
            blocks = dense[j, h].reshape(rows * 128, 128)
            right.append(jnp.concatenate([blocks, own_high, own_low, own_high], axis=0))
        return jnp.dot(left, jnp.concatenate(right, axis=1), preferred_element_type=jnp.float32)

    def next_state(step, j, scale):
        arrived = jnp.concatenate(
            [received[step, j, :, h].reshape(CROSS * half, 128) for h in range(2)], axis=1
        )
        total = ahead[...]
        for i in range(2):
            total += jnp.dot(crosser[i], arrived, preferred_element_type=jnp.float32)
        return scale * total - states[step, j]

    def arrive(step, j):
        for k in range(CROSS):
            exchange(step, j, k).wait_recv()

    @pl.loop(0, STEPS - 1)
    def _(step):
        scale = jnp.where(step == 0, 1.0, 2.0)

        def advance(j):
            arrive(step, j)
            state = next_state(step, j, scale)
            states[step + 2, j] = state
            keep(step + 1, j, state)

        ahead[...] = own_product(step, 0)

        @pl.loop(0, chunks - 1)
        def _(j):
            advance(j)
            ahead[...] = own_product(step, j + 1)
            send(step + 1, j)

        advance(chunks - 1)
        send(step + 1, chunks - 1)

    last = STEPS - 1
    ahead[...] = own_product(last, 0)

    @pl.loop(0, chunks - 1)
    def _(j):
        store(previous_out, j, states[STEPS, j])
        arrive(last, j)
        store(current_out, j, next_state(last, j, 2.0))
        ahead[...] = own_product(last, j + 1)

    store(previous_out, chunks - 1, states[STEPS, chunks - 1])
    arrive(last, chunks - 1)
    store(current_out, chunks - 1, next_state(last, chunks - 1, 2.0))

    @pl.loop(0, STEPS)
    def _(step):
        @pl.loop(0, chunks)
        def _(j):
            for k in range(CROSS):
                exchange(step, j, k).wait_send()


def leave(previous, current, previous_out, current_out, sem):
    copies = [
        pltpu.make_async_copy(previous, previous_out, sem.at[0]),
        pltpu.make_async_copy(current, current_out, sem.at[1]),
    ]
    for copy in copies:
        copy.start()
    for copy in copies:
        copy.wait()


def solution(mesh):
    wide_log = mesh.shape["wide"].bit_length() - 1
    narrow_log = mesh.shape["narrow"].bit_length() - 1

    def shards(initial, block_values, block_index, bond_sites, *rest):
        columns, width = initial.shape[2:]
        rows, kept = block_index.shape
        chunks = width // CHUNK
        sizes = (
            wide_log,
            narrow_log,
            columns,
            chunks,
            kept,
            bond_sites.shape[0],
            rest[1].shape[0],
        )
        whole = jax.ShapeDtypeStruct(initial.shape, jnp.float32)
        half_rows = CROSS * columns // 2
        smalls = (block_index, bond_sites.T, *rest)
        parts = pl.pallas_call(
            functools.partial(kernel, sizes),
            out_shape=(whole, whole),
            in_specs=[pl.BlockSpec(memory_space=pltpu.HBM)] * (2 + len(smalls)),
            out_specs=(pl.BlockSpec(memory_space=pltpu.VMEM),) * 2,
            scratch_shapes=[pltpu.SMEM(small.shape, small.dtype) for small in smalls]
            + [
                pltpu.VMEM((rows, kept + 1, 128, 128), jnp.bfloat16),
                pltpu.VMEM((chunks, 2, rows, 128, 128), jnp.bfloat16),
                pltpu.VMEM((STEPS + 1, chunks, columns, CHUNK), jnp.float32),
                pltpu.VMEM((STEPS, rows, columns, 128), jnp.bfloat16),
                pltpu.VMEM((STEPS, rows, columns, 128), jnp.bfloat16),
                pltpu.VMEM((columns, CHUNK), jnp.float32),
                pltpu.VMEM((STEPS, chunks, CROSS, 2, columns // 2, 128), jnp.bfloat16),
                pltpu.VMEM((STEPS, chunks, CROSS, 2, columns // 2, 128), jnp.bfloat16),
                pltpu.VMEM((columns, 3 * columns), jnp.bfloat16),
                pltpu.VMEM((2, columns, half_rows), jnp.bfloat16),
                pltpu.VMEM((half_rows, columns), jnp.bfloat16),
                pltpu.SemaphoreType.DMA((len(smalls),)),
                pltpu.SemaphoreType.DMA((chunks,)),
                pltpu.SemaphoreType.DMA((chunks,)),
                pltpu.SemaphoreType.DMA((STEPS, chunks, CROSS)),
                pltpu.SemaphoreType.DMA((STEPS, chunks, CROSS)),
            ],
            compiler_params=pltpu.CompilerParams(
                collective_id=0, has_side_effects=True, vmem_limit_bytes=48 * 1024 * 1024
            ),
        )(*[pltpu.with_memory_space_constraint(a, pltpu.HBM) for a in (initial, block_values, *smalls)])
        return pl.pallas_call(
            leave,
            out_shape=(whole, whole),
            in_specs=[pl.BlockSpec(memory_space=pl.ANY)] * 2,
            out_specs=(pl.BlockSpec(memory_space=pltpu.HBM),) * 2,
            scratch_shapes=[pltpu.SemaphoreType.DMA((2,))],
            compiler_params=pltpu.CompilerParams(vmem_limit_bytes=1024 * 1024),
        )(*parts)

    slab = P("wide", "narrow", None, None)
    return jax.shard_map(
        shards,
        mesh=mesh,
        in_specs=(slab,) + (P(),) * 10,
        out_specs=(slab, slab),
        check_vma=False,
    )
```

```python
import functools

import jax
import jax.numpy as jnp
from jax import lax
from jax.experimental import pallas as pl
from jax.experimental.pallas import tpu as pltpu
from jax.sharding import PartitionSpec as P

MESH = pl.DeviceIdType.MESH
STEPS = 4
CROSS = 4
CHUNK = 512
PARTS = CHUNK // 128


def bit_at(values, position):
    return jnp.bitwise_and(jnp.right_shift(values, position), 1)


def squeezed(columns, site):
    kept = jnp.bitwise_and(columns, jnp.left_shift(1, site) - 1)
    return kept | jnp.left_shift(jnp.right_shift(columns, site + 1), site)


def spread(packed, site, bit):
    kept = jnp.bitwise_and(packed, jnp.left_shift(1, site) - 1)
    high = jnp.left_shift(jnp.right_shift(packed, site), site + 1)
    return high | kept | jnp.left_shift(bit, site)


def lanes(count):
    return lax.broadcasted_iota(jnp.int32, (1, count), 1)


def rows_of(count, width):
    return lax.broadcasted_iota(jnp.int32, (count, width), 0)


def split(values):
    scaled = values * 65537.0
    high = scaled - (scaled - values)
    return high, values - high


def kernel(
    sizes,
    initial,
    block_values,
    *refs,
):
    smalls, (previous_out, current_out), refs = refs[:9], refs[9:11], refs[11:]
    (
        block_index,
        bond_sites,
        bond_coupling,
        pin_sites,
        pin_partner,
        pinned_spins,
        pin_coupling,
        cross_sites,
        cross_coupling,
    ) = refs[:9]
    (
        values,
        dense,
        states,
        high,
        low,
        ahead,
        sent,
        received,
        mixer,
        crosser,
        picker,
        small_sem,
        load_sem,
        value_sem,
        send_sem,
        recv_sem,
    ) = refs[9:]
    wide_log, narrow_log, columns, chunks, kept, bonds, pins = sizes
    rows = PARTS * chunks
    half = columns // 2
    wide, narrow = lax.axis_index("wide"), lax.axis_index("narrow")
    own_bits = (
        bit_at(wide, wide_log - 1),
        bit_at(wide, 0),
        bit_at(narrow, narrow_log - 1),
        bit_at(narrow, 0),
    )

    def flipped(index, bit, position):
        return index + (1 - 2 * bit) * (1 << position)

    partners = (
        (flipped(wide, own_bits[0], wide_log - 1), narrow),
        (flipped(wide, own_bits[1], 0), narrow),
        (wide, flipped(narrow, own_bits[2], narrow_log - 1)),
        (wide, flipped(narrow, own_bits[3], 0)),
    )
    barrier = pltpu.get_barrier_semaphore()
    for partner in partners:
        pl.semaphore_signal(barrier, inc=1, device_id=partner, device_id_type=MESH)

    def load_small(i):
        return pltpu.make_async_copy(smalls[i], refs[i], small_sem.at[i])

    def load(j):
        return pltpu.make_async_copy(
            initial.at[0, 0, :, pl.ds(pl.multiple_of(j * CHUNK, CHUNK), CHUNK)],
            states.at[1, j],
            load_sem.at[j],
        )

    def load_values(j):
        some = pl.ds(PARTS * j, PARTS)
        return pltpu.make_async_copy(
            block_values.at[some], values.at[some, pl.ds(0, kept)], value_sem.at[j]
        )

    def exchange(step, j, k):
        return pltpu.make_async_remote_copy(
            src_ref=sent.at[step, j, k],
            dst_ref=received.at[step, j, k],
            send_sem=send_sem.at[step, j, k],
            recv_sem=recv_sem.at[step, j, k],
            device_id=partners[k],
            device_id_type=MESH,
        )

    def store(out, j, state):
        out[0, 0, :, pl.ds(pl.multiple_of(j * CHUNK, CHUNK), CHUNK)] = state

    def keep(step, j, state):
        rounded = state.astype(jnp.bfloat16)
        rest = (state - rounded.astype(jnp.float32)).astype(jnp.bfloat16)
        packed = jnp.dot(picker[...], rounded, preferred_element_type=jnp.float32)
        packed = packed.astype(jnp.bfloat16)
        for h in range(PARTS):
            lanes_of = slice(h * 128, h * 128 + 128)
            high[step, PARTS * j + h] = rounded[:, lanes_of]
            low[step, PARTS * j + h] = rest[:, lanes_of]
            for k in range(CROSS):
                sent[step, j, k, h] = packed[k * half : k * half + half, lanes_of]

    def send(step, j):
        for k in range(CROSS):
            exchange(step, j, k).start()

    for i in range(9):
        load_small(i).start()
    for j in range(chunks):
        load(j).start()
    for j in range(chunks):
        load_values(j).start()
    for i in range(9):
        load_small(i).wait()

    sites = [cross_sites[k] for k in range(CROSS)]
    column = lanes(columns)
    for k in range(CROSS):
        places = jnp.where(
            bit_at(column, sites[k]) == own_bits[k], -1, squeezed(column, sites[k])
        )
        chosen = rows_of(half, columns) == places
        picker[k * half : k * half + half, :] = jnp.where(chosen, 1.0, 0.0).astype(jnp.bfloat16)

    pl.semaphore_wait(barrier, CROSS)

    @pl.loop(0, chunks)
    def _(j):
        load(j).wait()
        keep(0, j, states[1, j])
        send(0, j)

    crossing = [[], []]
    for pair in range(CROSS // 2):
        upper = lanes(columns) >= half
        one, two = 2 * pair, 2 * pair + 1

        def either(first, second):
            return jnp.where(upper, second, first)

        arriving = spread(
            jnp.bitwise_and(lanes(columns), half - 1),
            either(sites[one], sites[two]),
            either(1 - own_bits[one], 1 - own_bits[two]),
        )
        met = rows_of(columns, columns) == arriving
        strengths = zip(split(cross_coupling[one] * 0.5), split(cross_coupling[two] * 0.5))
        for part, (first, second) in zip(crossing, strengths):
            part.append(jnp.where(met, either(first, second), 0.0).astype(jnp.bfloat16))
    for i in range(2):
        crosser[i * columns : i * columns + columns, :] = jnp.concatenate(crossing[i], axis=1)

    row = rows_of(columns, columns)
    hopping = jnp.zeros((columns, columns), jnp.float32)
    diagonal = jnp.zeros((1, columns), jnp.float32)
    for b in range(bonds):
        one, two = bond_sites[0, b], bond_sites[1, b]
        differ = jnp.bitwise_xor(bit_at(column, one), bit_at(column, two)).astype(jnp.float32)
        source = jnp.bitwise_xor(column, jnp.left_shift(1, one) ^ jnp.left_shift(1, two))
        hopping += jnp.where(row == source, bond_coupling[b] * 0.5 * differ, 0.0)
        diagonal += bond_coupling[b] * 0.25 * (1.0 - 2.0 * differ)
    for p in range(pins):
        aligned = jnp.bitwise_xor(bit_at(column, pin_sites[p]), pinned_spins[pin_partner[p]])
        diagonal += pin_coupling[p] * 0.25 * (1.0 - 2.0 * aligned.astype(jnp.float32))
    for k in range(CROSS):
        parity = jnp.bitwise_xor(bit_at(column, sites[k]), own_bits[k])
        diagonal += cross_coupling[k] * 0.25 * (1.0 - 2.0 * parity.astype(jnp.float32))
    matrix = [
        part.astype(jnp.bfloat16) for part in split(hopping + jnp.where(row == column, diagonal, 0.0))
    ]
    mixer[...] = jnp.concatenate([matrix[0], matrix[0], matrix[1]], axis=1)
    states[0] = jnp.zeros(states.shape[1:], jnp.float32)
    values[:, kept] = jnp.zeros((rows, 128, 128), jnp.bfloat16)

    for j in range(chunks):
        load_values(j).wait()

    @pl.loop(0, chunks)
    def _(j):
        for part in range(PARTS):
            r = PARTS * j + part
            empty = sum(kept << 4 * i for i in range(8))
            places = [jnp.int32(empty - (1 << 32) if empty >> 31 else empty)] * 2
            for q in range(kept):
                wanted = block_index[r, q]
                shift = 4 * jnp.bitwise_and(wanted, 7)
                moved = jnp.left_shift(jnp.int32(q - kept), shift)
                upper = wanted >= 8
                places = [
                    places[0] + jnp.where(upper, 0, moved),
                    places[1] + jnp.where(upper, moved, 0),
                ]
            for m in range(rows):
                q = jnp.bitwise_and(jnp.right_shift(places[m // 8], 4 * (m % 8)), 15)
                dense[j, part, m] = values[r, jnp.minimum(q, kept)]

    def own_product(step, j):
        left = jnp.concatenate([high[step, m] for m in range(rows)] + [mixer[...]], axis=1)
        right = []
        for h in range(PARTS):
            own_high, own_low = high[step, PARTS * j + h], low[step, PARTS * j + h]
            blocks = dense[j, h].reshape(rows * 128, 128)
            right.append(jnp.concatenate([blocks, own_high, own_low, own_high], axis=0))
        return jnp.dot(left, jnp.concatenate(right, axis=1), preferred_element_type=jnp.float32)

    def crossing_product(step, j):
        arrived = jnp.concatenate(
            [received[step, j, :, h].reshape(CROSS * half, 128) for h in range(PARTS)], axis=1
        )
        both = jnp.dot(crosser[...], arrived, preferred_element_type=jnp.float32)
        return both[:columns] + both[columns:]

    def arrive(step, j):
        for k in range(CROSS):
            exchange(step, j, k).wait_recv()

    def next_state(step, j, scale):
        return scale * (ahead[...] + crossing_product(step, j)) - states[step, j]

    @pl.loop(0, STEPS - 1)
    def _(step):
        scale = jnp.where(step == 0, 1.0, 2.0)

        def advance(j):
            arrive(step, j)
            state = next_state(step, j, scale)
            states[step + 2, j] = state
            keep(step + 1, j, state)

        ahead[...] = own_product(step, 0)

        @pl.loop(0, chunks - 1)
        def _(j):
            advance(j)
            ahead[...] = own_product(step, j + 1)
            send(step + 1, j)

        advance(chunks - 1)
        send(step + 1, chunks - 1)

    last = STEPS - 1
    ahead[...] = own_product(last, 0)

    @pl.loop(0, chunks - 1)
    def _(j):
        store(previous_out, j, states[STEPS, j])
        arrive(last, j)
        store(current_out, j, next_state(last, j, 2.0))
        ahead[...] = own_product(last, j + 1)

    store(previous_out, chunks - 1, states[STEPS, chunks - 1])
    arrive(last, chunks - 1)
    store(current_out, chunks - 1, next_state(last, chunks - 1, 2.0))

    @pl.loop(0, STEPS)
    def _(step):
        @pl.loop(0, chunks)
        def _(j):
            for k in range(CROSS):
                exchange(step, j, k).wait_send()


def leave(previous, current, previous_out, current_out, sem):
    copies = [
        pltpu.make_async_copy(previous, previous_out, sem.at[0]),
        pltpu.make_async_copy(current, current_out, sem.at[1]),
    ]
    for copy in copies:
        copy.start()
    for copy in copies:
        copy.wait()


def solution(mesh):
    wide_log = mesh.shape["wide"].bit_length() - 1
    narrow_log = mesh.shape["narrow"].bit_length() - 1

    def shards(initial, block_values, block_index, bond_sites, *rest):
        columns, width = initial.shape[2:]
        rows, kept = block_index.shape
        chunks = width // CHUNK
        sizes = (
            wide_log,
            narrow_log,
            columns,
            chunks,
            kept,
            bond_sites.shape[0],
            rest[1].shape[0],
        )
        whole = jax.ShapeDtypeStruct(initial.shape, jnp.float32)
        half_rows = CROSS * columns // 2
        smalls = (block_index, bond_sites.T, *rest)
        parts = pl.pallas_call(
            functools.partial(kernel, sizes),
            out_shape=(whole, whole),
            in_specs=[pl.BlockSpec(memory_space=pltpu.HBM)] * (2 + len(smalls)),
            out_specs=(pl.BlockSpec(memory_space=pltpu.VMEM),) * 2,
            scratch_shapes=[pltpu.SMEM(small.shape, small.dtype) for small in smalls]
            + [
                pltpu.VMEM((rows, kept + 1, 128, 128), jnp.bfloat16),
                pltpu.VMEM((chunks, PARTS, rows, 128, 128), jnp.bfloat16),
                pltpu.VMEM((STEPS + 1, chunks, columns, CHUNK), jnp.float32),
                pltpu.VMEM((STEPS, rows, columns, 128), jnp.bfloat16),
                pltpu.VMEM((STEPS, rows, columns, 128), jnp.bfloat16),
                pltpu.VMEM((columns, CHUNK), jnp.float32),
                pltpu.VMEM((STEPS, chunks, CROSS, PARTS, columns // 2, 128), jnp.bfloat16),
                pltpu.VMEM((STEPS, chunks, CROSS, PARTS, columns // 2, 128), jnp.bfloat16),
                pltpu.VMEM((columns, 3 * columns), jnp.bfloat16),
                pltpu.VMEM((2 * columns, half_rows), jnp.bfloat16),
                pltpu.VMEM((half_rows, columns), jnp.bfloat16),
                pltpu.SemaphoreType.DMA((len(smalls),)),
                pltpu.SemaphoreType.DMA((chunks,)),
                pltpu.SemaphoreType.DMA((chunks,)),
                pltpu.SemaphoreType.DMA((STEPS, chunks, CROSS)),
                pltpu.SemaphoreType.DMA((STEPS, chunks, CROSS)),
            ],
            compiler_params=pltpu.CompilerParams(
                collective_id=0, has_side_effects=True, vmem_limit_bytes=48 * 1024 * 1024
            ),
        )(*[pltpu.with_memory_space_constraint(a, pltpu.HBM) for a in (initial, block_values, *smalls)])
        return pl.pallas_call(
            leave,
            out_shape=(whole, whole),
            in_specs=[pl.BlockSpec(memory_space=pl.ANY)] * 2,
            out_specs=(pl.BlockSpec(memory_space=pltpu.HBM),) * 2,
            scratch_shapes=[pltpu.SemaphoreType.DMA((2,))],
            compiler_params=pltpu.CompilerParams(vmem_limit_bytes=1024 * 1024),
        )(*parts)

    slab = P("wide", "narrow", None, None)
    return jax.shard_map(
        shards,
        mesh=mesh,
        in_specs=(slab,) + (P(),) * 10,
        out_specs=(slab, slab),
        check_vma=False,
    )
```

```python
import functools

import jax
import jax.numpy as jnp
from jax import lax
from jax.experimental import pallas as pl
from jax.experimental.pallas import tpu as pltpu
from jax.sharding import PartitionSpec as P

MESH = pl.DeviceIdType.MESH
STEPS = 4
CROSS = 4
CHUNK = 512
PARTS = CHUNK // 128
EARLY = 8


def bit_at(values, position):
    return jnp.bitwise_and(jnp.right_shift(values, position), 1)


def squeezed(columns, site):
    kept = jnp.bitwise_and(columns, jnp.left_shift(1, site) - 1)
    return kept | jnp.left_shift(jnp.right_shift(columns, site + 1), site)


def spread(packed, site, bit):
    kept = jnp.bitwise_and(packed, jnp.left_shift(1, site) - 1)
    high = jnp.left_shift(jnp.right_shift(packed, site), site + 1)
    return high | kept | jnp.left_shift(bit, site)


def lanes(count):
    return lax.broadcasted_iota(jnp.int32, (1, count), 1)


def rows_of(count, width):
    return lax.broadcasted_iota(jnp.int32, (count, width), 0)


def split(values):
    scaled = values * 65537.0
    high = scaled - (scaled - values)
    return high, values - high


def kernel(
    sizes,
    initial,
    block_values,
    *refs,
):
    smalls, (previous_out, current_out), refs = refs[:9], refs[9:11], refs[11:]
    (
        block_index,
        bond_sites,
        bond_coupling,
        pin_sites,
        pin_partner,
        pinned_spins,
        pin_coupling,
        cross_sites,
        cross_coupling,
    ) = refs[:9]
    (
        values,
        dense,
        states,
        high,
        low,
        ahead,
        sent,
        received,
        mixer,
        crosser,
        picker,
        small_sem,
        load_sem,
        value_sem,
        send_sem,
        recv_sem,
    ) = refs[9:]
    wide_log, narrow_log, columns, chunks, kept, bonds, pins = sizes
    rows = PARTS * chunks
    half = columns // 2
    wide, narrow = lax.axis_index("wide"), lax.axis_index("narrow")
    own_bits = (
        bit_at(wide, wide_log - 1),
        bit_at(wide, 0),
        bit_at(narrow, narrow_log - 1),
        bit_at(narrow, 0),
    )

    def flipped(index, bit, position):
        return index + (1 - 2 * bit) * (1 << position)

    partners = (
        (flipped(wide, own_bits[0], wide_log - 1), narrow),
        (flipped(wide, own_bits[1], 0), narrow),
        (wide, flipped(narrow, own_bits[2], narrow_log - 1)),
        (wide, flipped(narrow, own_bits[3], 0)),
    )
    barrier = pltpu.get_barrier_semaphore()
    for partner in partners:
        pl.semaphore_signal(barrier, inc=1, device_id=partner, device_id_type=MESH)

    def load_small(i):
        return pltpu.make_async_copy(smalls[i], refs[i], small_sem.at[i])

    def load(j):
        return pltpu.make_async_copy(
            initial.at[0, 0, :, pl.ds(pl.multiple_of(j * CHUNK, CHUNK), CHUNK)],
            states.at[1, j],
            load_sem.at[j],
        )

    def load_values(j):
        some = pl.ds(PARTS * j, PARTS)
        return pltpu.make_async_copy(
            block_values.at[some], values.at[some, pl.ds(0, kept)], value_sem.at[0]
        )

    def exchange(step, j, k):
        return pltpu.make_async_remote_copy(
            src_ref=sent.at[step, j, k],
            dst_ref=received.at[step, j, k],
            send_sem=send_sem.at[step],
            recv_sem=recv_sem.at[lax.rem(step, 2), j],
            device_id=partners[k],
            device_id_type=MESH,
        )

    def arrival(step, j):
        every = received.at[step, j]
        return pltpu.make_async_copy(every, every, recv_sem.at[lax.rem(step, 2), j])

    def departure(step):
        every = sent.at[step]
        return pltpu.make_async_copy(every, every, send_sem.at[step])

    def store(out, j, state):
        out[0, 0, :, pl.ds(pl.multiple_of(j * CHUNK, CHUNK), CHUNK)] = state

    def keep(step, j, state):
        rounded = state.astype(jnp.bfloat16)
        rest = (state - rounded.astype(jnp.float32)).astype(jnp.bfloat16)
        packed = jnp.dot(picker[...], rounded, preferred_element_type=jnp.float32)
        packed = packed.astype(jnp.bfloat16)
        for h in range(PARTS):
            lanes_of = slice(h * 128, h * 128 + 128)
            high[step, PARTS * j + h] = rounded[:, lanes_of]
            low[step, PARTS * j + h] = rest[:, lanes_of]
            for k in range(CROSS):
                sent[step, j, k, h] = packed[k * half : k * half + half, lanes_of]

    def send(step, j):
        for k in range(CROSS):
            exchange(step, j, k).start()

    for i in range(9):
        load_small(i).start()
    for j in range(chunks):
        load(j).start()
    for j in range(chunks):
        load_values(j).start()
    for i in range(9):
        load_small(i).wait()

    sites = [cross_sites[k] for k in range(CROSS)]
    column = lanes(columns)
    for k in range(CROSS):
        places = jnp.where(
            bit_at(column, sites[k]) == own_bits[k], -1, squeezed(column, sites[k])
        )
        chosen = rows_of(half, columns) == places
        picker[k * half : k * half + half, :] = jnp.where(chosen, 1.0, 0.0).astype(jnp.bfloat16)

    pl.semaphore_wait(barrier, CROSS)

    @pl.loop(0, chunks)
    def _(j):
        load(j).wait()
        keep(0, j, states[1, j])
        send(0, j)

    crossing = [[], []]
    for pair in range(CROSS // 2):
        upper = lanes(columns) >= half
        one, two = 2 * pair, 2 * pair + 1

        def either(first, second):
            return jnp.where(upper, second, first)

        arriving = spread(
            jnp.bitwise_and(lanes(columns), half - 1),
            either(sites[one], sites[two]),
            either(1 - own_bits[one], 1 - own_bits[two]),
        )
        met = rows_of(columns, columns) == arriving
        strengths = zip(split(cross_coupling[one] * 0.5), split(cross_coupling[two] * 0.5))
        for part, (first, second) in zip(crossing, strengths):
            part.append(jnp.where(met, either(first, second), 0.0).astype(jnp.bfloat16))
    for i in range(2):
        crosser[i * columns : i * columns + columns, :] = jnp.concatenate(crossing[i], axis=1)

    row = rows_of(columns, columns)
    hopping = jnp.zeros((columns, columns), jnp.float32)
    diagonal = jnp.zeros((1, columns), jnp.float32)
    for b in range(bonds):
        one, two = bond_sites[0, b], bond_sites[1, b]
        differ = jnp.bitwise_xor(bit_at(column, one), bit_at(column, two)).astype(jnp.float32)
        source = jnp.bitwise_xor(column, jnp.left_shift(1, one) ^ jnp.left_shift(1, two))
        hopping += jnp.where(row == source, bond_coupling[b] * 0.5 * differ, 0.0)
        diagonal += bond_coupling[b] * 0.25 * (1.0 - 2.0 * differ)
    for p in range(pins):
        aligned = jnp.bitwise_xor(bit_at(column, pin_sites[p]), pinned_spins[pin_partner[p]])
        diagonal += pin_coupling[p] * 0.25 * (1.0 - 2.0 * aligned.astype(jnp.float32))
    for k in range(CROSS):
        parity = jnp.bitwise_xor(bit_at(column, sites[k]), own_bits[k])
        diagonal += cross_coupling[k] * 0.25 * (1.0 - 2.0 * parity.astype(jnp.float32))
    matrix = [
        part.astype(jnp.bfloat16) for part in split(hopping + jnp.where(row == column, diagonal, 0.0))
    ]
    mixer[...] = jnp.concatenate([matrix[0], matrix[0], matrix[1]], axis=1)
    states[0] = jnp.zeros(states.shape[1:], jnp.float32)
    values[:, kept] = jnp.zeros((rows, 128, 128), jnp.bfloat16)

    every = values.at[:, pl.ds(0, kept)]
    pltpu.make_async_copy(every, every, value_sem.at[0]).wait()

    @pl.loop(0, chunks)
    def _(j):
        for part in range(PARTS):
            r = PARTS * j + part
            empty = sum(kept << 4 * i for i in range(8))
            places = [jnp.int32(empty - (1 << 32) if empty >> 31 else empty)] * 2
            for q in range(kept):
                wanted = block_index[r, q]
                shift = 4 * jnp.bitwise_and(wanted, 7)
                moved = jnp.left_shift(jnp.int32(q - kept), shift)
                upper = wanted >= 8
                places = [
                    places[0] + jnp.where(upper, 0, moved),
                    places[1] + jnp.where(upper, moved, 0),
                ]
            for m in range(rows):
                q = jnp.bitwise_and(jnp.right_shift(places[m // 8], 4 * (m % 8)), 15)
                dense[j, part, m] = values[r, jnp.minimum(q, kept)]

    def own_product(step, j, first, count, column):
        left = [high[step, first + m] for m in range(count)]
        if column:
            left.append(mixer[...])
        right = []
        for h in range(PARTS):
            blocks = [dense[j, h, first : first + count].reshape(count * 128, 128)]
            if column:
                own_high, own_low = high[step, PARTS * j + h], low[step, PARTS * j + h]
                blocks += [own_high, own_low, own_high]
            right.append(jnp.concatenate(blocks, axis=0))
        return jnp.dot(
            jnp.concatenate(left, axis=1),
            jnp.concatenate(right, axis=1),
            preferred_element_type=jnp.float32,
        )

    def crossing_product(step, j):
        arrived = jnp.concatenate(
            [received[step, j, :, h].reshape(CROSS * half, 128) for h in range(PARTS)], axis=1
        )
        both = jnp.dot(crosser[...], arrived, preferred_element_type=jnp.float32)
        return both[:columns] + both[columns:]

    def arrive(step, j):
        arrival(step, j).wait()

    def next_state(step, j, scale):
        return scale * (ahead[...] + crossing_product(step, j)) - states[step, j]

    ahead[...] = own_product(0, 0, 0, rows, True)

    @pl.loop(0, STEPS - 1)
    def _(step):
        scale = jnp.where(step == 0, 1.0, 2.0)

        def advance(j):
            arrive(step, j)
            state = next_state(step, j, scale)
            states[step + 2, j] = state
            keep(step + 1, j, state)

        @pl.loop(0, chunks - 1)
        def _(j):
            advance(j)
            ahead[...] = own_product(step, j + 1, 0, EARLY, True)
            send(step + 1, j)
            ahead[...] += own_product(step, j + 1, EARLY, rows - EARLY, False)

        advance(chunks - 1)
        ahead[...] = own_product(step + 1, 0, 0, rows - PARTS, True)
        send(step + 1, chunks - 1)
        ahead[...] += own_product(step + 1, 0, rows - PARTS, PARTS, False)

    last = STEPS - 1

    @pl.loop(0, chunks - 1)
    def _(j):
        store(previous_out, j, states[STEPS, j])
        arrive(last, j)
        store(current_out, j, next_state(last, j, 2.0))
        ahead[...] = own_product(last, j + 1, 0, rows, True)

    store(previous_out, chunks - 1, states[STEPS, chunks - 1])
    arrive(last, chunks - 1)
    store(current_out, chunks - 1, next_state(last, chunks - 1, 2.0))

    for step in range(STEPS):
        departure(step).wait()


def leave(previous, current, previous_out, current_out, sem):
    copies = [
        pltpu.make_async_copy(previous, previous_out, sem.at[0]),
        pltpu.make_async_copy(current, current_out, sem.at[1]),
    ]
    for copy in copies:
        copy.start()
    for copy in copies:
        copy.wait()


def solution(mesh):
    wide_log = mesh.shape["wide"].bit_length() - 1
    narrow_log = mesh.shape["narrow"].bit_length() - 1

    def shards(initial, block_values, block_index, bond_sites, *rest):
        columns, width = initial.shape[2:]
        rows, kept = block_index.shape
        chunks = width // CHUNK
        sizes = (
            wide_log,
            narrow_log,
            columns,
            chunks,
            kept,
            bond_sites.shape[0],
            rest[1].shape[0],
        )
        whole = jax.ShapeDtypeStruct(initial.shape, jnp.float32)
        half_rows = CROSS * columns // 2
        smalls = (block_index, bond_sites.T, *rest)
        parts = pl.pallas_call(
            functools.partial(kernel, sizes),
            out_shape=(whole, whole),
            in_specs=[pl.BlockSpec(memory_space=pltpu.HBM)] * (2 + len(smalls)),
            out_specs=(pl.BlockSpec(memory_space=pltpu.VMEM),) * 2,
            scratch_shapes=[pltpu.SMEM(small.shape, small.dtype) for small in smalls]
            + [
                pltpu.VMEM((rows, kept + 1, 128, 128), jnp.bfloat16),
                pltpu.VMEM((chunks, PARTS, rows, 128, 128), jnp.bfloat16),
                pltpu.VMEM((STEPS + 1, chunks, columns, CHUNK), jnp.float32),
                pltpu.VMEM((STEPS, rows, columns, 128), jnp.bfloat16),
                pltpu.VMEM((STEPS, rows, columns, 128), jnp.bfloat16),
                pltpu.VMEM((columns, CHUNK), jnp.float32),
                pltpu.VMEM((STEPS, chunks, CROSS, PARTS, columns // 2, 128), jnp.bfloat16),
                pltpu.VMEM((STEPS, chunks, CROSS, PARTS, columns // 2, 128), jnp.bfloat16),
                pltpu.VMEM((columns, 3 * columns), jnp.bfloat16),
                pltpu.VMEM((2 * columns, half_rows), jnp.bfloat16),
                pltpu.VMEM((half_rows, columns), jnp.bfloat16),
                pltpu.SemaphoreType.DMA((len(smalls),)),
                pltpu.SemaphoreType.DMA((chunks,)),
                pltpu.SemaphoreType.DMA((1,)),
                pltpu.SemaphoreType.DMA((STEPS,)),
                pltpu.SemaphoreType.DMA((2, chunks)),
            ],
            compiler_params=pltpu.CompilerParams(
                collective_id=0, has_side_effects=True, vmem_limit_bytes=48 * 1024 * 1024
            ),
        )(*[pltpu.with_memory_space_constraint(a, pltpu.HBM) for a in (initial, block_values, *smalls)])
        return pl.pallas_call(
            leave,
            out_shape=(whole, whole),
            in_specs=[pl.BlockSpec(memory_space=pl.ANY)] * 2,
            out_specs=(pl.BlockSpec(memory_space=pltpu.HBM),) * 2,
            scratch_shapes=[pltpu.SemaphoreType.DMA((2,))],
            compiler_params=pltpu.CompilerParams(vmem_limit_bytes=1024 * 1024),
        )(*parts)

    slab = P("wide", "narrow", None, None)
    return jax.shard_map(
        shards,
        mesh=mesh,
        in_specs=(slab,) + (P(),) * 10,
        out_specs=(slab, slab),
        check_vma=False,
    )
```

```python
import functools

import jax
import jax.numpy as jnp
from jax import lax
from jax.experimental import pallas as pl
from jax.experimental.pallas import tpu as pltpu
from jax.sharding import PartitionSpec as P

MESH = pl.DeviceIdType.MESH
STEPS = 4
CROSS = 4
CHUNK = 512
PARTS = CHUNK // 128
EARLY = 8


def bit_at(values, position):
    return jnp.bitwise_and(jnp.right_shift(values, position), 1)


def squeezed(columns, site):
    kept = jnp.bitwise_and(columns, jnp.left_shift(1, site) - 1)
    return kept | jnp.left_shift(jnp.right_shift(columns, site + 1), site)


def spread(packed, site, bit):
    kept = jnp.bitwise_and(packed, jnp.left_shift(1, site) - 1)
    high = jnp.left_shift(jnp.right_shift(packed, site), site + 1)
    return high | kept | jnp.left_shift(bit, site)


def lanes(count):
    return lax.broadcasted_iota(jnp.int32, (1, count), 1)


def rows_of(count, width):
    return lax.broadcasted_iota(jnp.int32, (count, width), 0)


def split(values):
    scaled = values * 65537.0
    high = scaled - (scaled - values)
    return high, values - high


def kernel(
    sizes,
    initial,
    block_values,
    *refs,
):
    smalls, (previous_out, current_out), refs = refs[:9], refs[9:11], refs[11:]
    (
        block_index,
        bond_sites,
        bond_coupling,
        pin_sites,
        pin_partner,
        pinned_spins,
        pin_coupling,
        cross_sites,
        cross_coupling,
    ) = refs[:9]
    (
        values,
        dense,
        states,
        high,
        low,
        ahead,
        sent,
        received,
        mixer,
        crosser,
        picker,
        small_sem,
        load_sem,
        value_sem,
        send_sem,
        recv_sem,
    ) = refs[9:]
    wide_log, narrow_log, columns, chunks, kept, bonds, pins = sizes
    rows = PARTS * chunks
    half = columns // 2
    wide, narrow = lax.axis_index("wide"), lax.axis_index("narrow")
    own_bits = (
        bit_at(wide, wide_log - 1),
        bit_at(wide, 0),
        bit_at(narrow, narrow_log - 1),
        bit_at(narrow, 0),
    )

    def flipped(index, bit, position):
        return index + (1 - 2 * bit) * (1 << position)

    partners = (
        (flipped(wide, own_bits[0], wide_log - 1), narrow),
        (flipped(wide, own_bits[1], 0), narrow),
        (wide, flipped(narrow, own_bits[2], narrow_log - 1)),
        (wide, flipped(narrow, own_bits[3], 0)),
    )
    barrier = pltpu.get_barrier_semaphore()
    for partner in partners:
        pl.semaphore_signal(barrier, inc=1, device_id=partner, device_id_type=MESH)

    def load_small(i):
        return pltpu.make_async_copy(smalls[i], refs[i], small_sem.at[i])

    def load(j):
        return pltpu.make_async_copy(
            initial.at[0, 0, :, pl.ds(pl.multiple_of(j * CHUNK, CHUNK), CHUNK)],
            states.at[1, j],
            load_sem.at[j],
        )

    def load_values(j):
        some = pl.ds(PARTS * j, PARTS)
        return pltpu.make_async_copy(
            block_values.at[some], values.at[some, pl.ds(0, kept)], value_sem.at[0]
        )

    def exchange(step, j, k):
        return pltpu.make_async_remote_copy(
            src_ref=sent.at[step, j, k],
            dst_ref=received.at[step, j, k],
            send_sem=send_sem.at[step],
            recv_sem=recv_sem.at[lax.rem(step, 2), j],
            device_id=partners[k],
            device_id_type=MESH,
        )

    def arrival(step, j):
        every = received.at[step, j]
        return pltpu.make_async_copy(every, every, recv_sem.at[lax.rem(step, 2), j])

    def departure(step):
        every = sent.at[step]
        return pltpu.make_async_copy(every, every, send_sem.at[step])

    def store(out, j, state):
        out[0, 0, :, pl.ds(pl.multiple_of(j * CHUNK, CHUNK), CHUNK)] = state

    def keep(step, j, state):
        rounded = state.astype(jnp.bfloat16)
        rest = (state - rounded.astype(jnp.float32)).astype(jnp.bfloat16)
        packed = jnp.dot(picker[...], rounded, preferred_element_type=jnp.float32)
        packed = packed.astype(jnp.bfloat16)
        for h in range(PARTS):
            lanes_of = slice(h * 128, h * 128 + 128)
            high[step, PARTS * j + h] = rounded[:, lanes_of]
            low[step, PARTS * j + h] = rest[:, lanes_of]
            for k in range(CROSS):
                sent[step, j, k, h] = packed[k * half : k * half + half, lanes_of]

    def send(step, j):
        for k in range(CROSS):
            exchange(step, j, k).start()

    load_small(7).start()
    for j in range(chunks):
        load(j).start()
    others = [i for i in range(9) if i != 7]
    for i in others:
        load_small(i).start()
    for j in range(chunks):
        load_values(j).start()
    load_small(7).wait()

    sites = [cross_sites[k] for k in range(CROSS)]
    column = lanes(columns)
    for k in range(CROSS):
        places = jnp.where(
            bit_at(column, sites[k]) == own_bits[k], -1, squeezed(column, sites[k])
        )
        chosen = rows_of(half, columns) == places
        picker[k * half : k * half + half, :] = jnp.where(chosen, 1.0, 0.0).astype(jnp.bfloat16)

    pl.semaphore_wait(barrier, CROSS)

    @pl.loop(0, chunks)
    def _(j):
        load(j).wait()
        keep(0, j, states[1, j])
        send(0, j)

    for i in others:
        load_small(i).wait()
    crossing = [[], []]
    for pair in range(CROSS // 2):
        upper = lanes(columns) >= half
        one, two = 2 * pair, 2 * pair + 1

        def either(first, second):
            return jnp.where(upper, second, first)

        arriving = spread(
            jnp.bitwise_and(lanes(columns), half - 1),
            either(sites[one], sites[two]),
            either(1 - own_bits[one], 1 - own_bits[two]),
        )
        met = rows_of(columns, columns) == arriving
        strengths = zip(split(cross_coupling[one] * 0.5), split(cross_coupling[two] * 0.5))
        for part, (first, second) in zip(crossing, strengths):
            part.append(jnp.where(met, either(first, second), 0.0).astype(jnp.bfloat16))
    for i in range(2):
        crosser[i * columns : i * columns + columns, :] = jnp.concatenate(crossing[i], axis=1)

    row = rows_of(columns, columns)
    hopping = jnp.zeros((columns, columns), jnp.float32)
    diagonal = jnp.zeros((1, columns), jnp.float32)
    for b in range(bonds):
        one, two = bond_sites[0, b], bond_sites[1, b]
        differ = jnp.bitwise_xor(bit_at(column, one), bit_at(column, two)).astype(jnp.float32)
        source = jnp.bitwise_xor(column, jnp.left_shift(1, one) ^ jnp.left_shift(1, two))
        hopping += jnp.where(row == source, bond_coupling[b] * 0.5 * differ, 0.0)
        diagonal += bond_coupling[b] * 0.25 * (1.0 - 2.0 * differ)
    for p in range(pins):
        aligned = jnp.bitwise_xor(bit_at(column, pin_sites[p]), pinned_spins[pin_partner[p]])
        diagonal += pin_coupling[p] * 0.25 * (1.0 - 2.0 * aligned.astype(jnp.float32))
    for k in range(CROSS):
        parity = jnp.bitwise_xor(bit_at(column, sites[k]), own_bits[k])
        diagonal += cross_coupling[k] * 0.25 * (1.0 - 2.0 * parity.astype(jnp.float32))
    matrix = [
        part.astype(jnp.bfloat16) for part in split(hopping + jnp.where(row == column, diagonal, 0.0))
    ]
    mixer[...] = jnp.concatenate([matrix[0], matrix[0], matrix[1]], axis=1)
    states[0] = jnp.zeros(states.shape[1:], jnp.float32)
    values[:, kept] = jnp.zeros((rows, 128, 128), jnp.bfloat16)

    every = values.at[:, pl.ds(0, kept)]
    pltpu.make_async_copy(every, every, value_sem.at[0]).wait()

    @pl.loop(0, chunks)
    def _(j):
        for part in range(PARTS):
            r = PARTS * j + part
            empty = sum(kept << 4 * i for i in range(8))
            places = [jnp.int32(empty - (1 << 32) if empty >> 31 else empty)] * 2
            for q in range(kept):
                wanted = block_index[r, q]
                shift = 4 * jnp.bitwise_and(wanted, 7)
                moved = jnp.left_shift(jnp.int32(q - kept), shift)
                upper = wanted >= 8
                places = [
                    places[0] + jnp.where(upper, 0, moved),
                    places[1] + jnp.where(upper, moved, 0),
                ]
            for m in range(rows):
                q = jnp.bitwise_and(jnp.right_shift(places[m // 8], 4 * (m % 8)), 15)
                dense[j, part, m] = values[r, jnp.minimum(q, kept)]

    def own_product(step, j, first, count, column):
        left = [high[step, first + m] for m in range(count)]
        if column:
            left.append(mixer[...])
        right = []
        for h in range(PARTS):
            blocks = [dense[j, h, first : first + count].reshape(count * 128, 128)]
            if column:
                own_high, own_low = high[step, PARTS * j + h], low[step, PARTS * j + h]
                blocks += [own_high, own_low, own_high]
            right.append(jnp.concatenate(blocks, axis=0))
        return jnp.dot(
            jnp.concatenate(left, axis=1),
            jnp.concatenate(right, axis=1),
            preferred_element_type=jnp.float32,
        )

    def crossing_product(step, j):
        arrived = jnp.concatenate(
            [received[step, j, :, h].reshape(CROSS * half, 128) for h in range(PARTS)], axis=1
        )
        both = jnp.dot(crosser[...], arrived, preferred_element_type=jnp.float32)
        return both[:columns] + both[columns:]

    def arrive(step, j):
        arrival(step, j).wait()

    def next_state(step, j, scale):
        return scale * (ahead[...] + crossing_product(step, j)) - states[step, j]

    ahead[...] = own_product(0, 0, 0, rows, True)

    @pl.loop(0, STEPS - 1)
    def _(step):
        scale = jnp.where(step == 0, 1.0, 2.0)

        def advance(j):
            arrive(step, j)
            state = next_state(step, j, scale)
            states[step + 2, j] = state
            keep(step + 1, j, state)

        @pl.loop(0, chunks - 1)
        def _(j):
            advance(j)
            ahead[...] = own_product(step, j + 1, 0, EARLY, True)
            send(step + 1, j)
            ahead[...] += own_product(step, j + 1, EARLY, rows - EARLY, False)

        advance(chunks - 1)
        ahead[...] = own_product(step + 1, 0, 0, rows - PARTS, True)
        send(step + 1, chunks - 1)
        ahead[...] += own_product(step + 1, 0, rows - PARTS, PARTS, False)

    last = STEPS - 1

    @pl.loop(0, chunks - 1)
    def _(j):
        store(previous_out, j, states[STEPS, j])
        arrive(last, j)
        store(current_out, j, next_state(last, j, 2.0))
        ahead[...] = own_product(last, j + 1, 0, rows, True)

    store(previous_out, chunks - 1, states[STEPS, chunks - 1])
    arrive(last, chunks - 1)
    store(current_out, chunks - 1, next_state(last, chunks - 1, 2.0))

    for step in range(STEPS):
        departure(step).wait()


def leave(previous, current, previous_out, current_out, sem):
    copies = [
        pltpu.make_async_copy(previous, previous_out, sem.at[0]),
        pltpu.make_async_copy(current, current_out, sem.at[1]),
    ]
    for copy in copies:
        copy.start()
    for copy in copies:
        copy.wait()


def solution(mesh):
    wide_log = mesh.shape["wide"].bit_length() - 1
    narrow_log = mesh.shape["narrow"].bit_length() - 1

    def shards(initial, block_values, block_index, bond_sites, *rest):
        columns, width = initial.shape[2:]
        rows, kept = block_index.shape
        chunks = width // CHUNK
        sizes = (
            wide_log,
            narrow_log,
            columns,
            chunks,
            kept,
            bond_sites.shape[0],
            rest[1].shape[0],
        )
        whole = jax.ShapeDtypeStruct(initial.shape, jnp.float32)
        half_rows = CROSS * columns // 2
        smalls = (block_index, bond_sites.T, *rest)
        parts = pl.pallas_call(
            functools.partial(kernel, sizes),
            out_shape=(whole, whole),
            in_specs=[pl.BlockSpec(memory_space=pltpu.HBM)] * (2 + len(smalls)),
            out_specs=(pl.BlockSpec(memory_space=pltpu.VMEM),) * 2,
            scratch_shapes=[pltpu.SMEM(small.shape, small.dtype) for small in smalls]
            + [
                pltpu.VMEM((rows, kept + 1, 128, 128), jnp.bfloat16),
                pltpu.VMEM((chunks, PARTS, rows, 128, 128), jnp.bfloat16),
                pltpu.VMEM((STEPS + 1, chunks, columns, CHUNK), jnp.float32),
                pltpu.VMEM((STEPS, rows, columns, 128), jnp.bfloat16),
                pltpu.VMEM((STEPS, rows, columns, 128), jnp.bfloat16),
                pltpu.VMEM((columns, CHUNK), jnp.float32),
                pltpu.VMEM((STEPS, chunks, CROSS, PARTS, columns // 2, 128), jnp.bfloat16),
                pltpu.VMEM((STEPS, chunks, CROSS, PARTS, columns // 2, 128), jnp.bfloat16),
                pltpu.VMEM((columns, 3 * columns), jnp.bfloat16),
                pltpu.VMEM((2 * columns, half_rows), jnp.bfloat16),
                pltpu.VMEM((half_rows, columns), jnp.bfloat16),
                pltpu.SemaphoreType.DMA((len(smalls),)),
                pltpu.SemaphoreType.DMA((chunks,)),
                pltpu.SemaphoreType.DMA((1,)),
                pltpu.SemaphoreType.DMA((STEPS,)),
                pltpu.SemaphoreType.DMA((2, chunks)),
            ],
            compiler_params=pltpu.CompilerParams(
                collective_id=0, has_side_effects=True, vmem_limit_bytes=48 * 1024 * 1024
            ),
        )(*[pltpu.with_memory_space_constraint(a, pltpu.HBM) for a in (initial, block_values, *smalls)])
        return pl.pallas_call(
            leave,
            out_shape=(whole, whole),
            in_specs=[pl.BlockSpec(memory_space=pl.ANY)] * 2,
            out_specs=(pl.BlockSpec(memory_space=pltpu.HBM),) * 2,
            scratch_shapes=[pltpu.SemaphoreType.DMA((2,))],
            compiler_params=pltpu.CompilerParams(vmem_limit_bytes=1024 * 1024),
        )(*parts)

    slab = P("wide", "narrow", None, None)
    return jax.shard_map(
        shards,
        mesh=mesh,
        in_specs=(slab,) + (P(),) * 10,
        out_specs=(slab, slab),
        check_vma=False,
    )
```

```python
import functools

import jax
import jax.numpy as jnp
from jax import lax
from jax.experimental import pallas as pl
from jax.experimental.pallas import tpu as pltpu
from jax.sharding import PartitionSpec as P

MESH = pl.DeviceIdType.MESH
STEPS = 4
CROSS = 4
CHUNK = 512
PARTS = CHUNK // 128
EARLY = 8


def bit_at(values, position):
    return jnp.bitwise_and(jnp.right_shift(values, position), 1)


def squeezed(columns, site):
    kept = jnp.bitwise_and(columns, jnp.left_shift(1, site) - 1)
    return kept | jnp.left_shift(jnp.right_shift(columns, site + 1), site)


def spread(packed, site, bit):
    kept = jnp.bitwise_and(packed, jnp.left_shift(1, site) - 1)
    high = jnp.left_shift(jnp.right_shift(packed, site), site + 1)
    return high | kept | jnp.left_shift(bit, site)


def lanes(count):
    return lax.broadcasted_iota(jnp.int32, (1, count), 1)


def rows_of(count, width):
    return lax.broadcasted_iota(jnp.int32, (count, width), 0)


def split(values):
    scaled = values * 65537.0
    high = scaled - (scaled - values)
    return high, values - high


def kernel(
    sizes,
    initial,
    block_values,
    *refs,
):
    smalls, (previous_out, current_out), refs = refs[:9], refs[9:11], refs[11:]
    (
        block_index,
        bond_sites,
        bond_coupling,
        pin_sites,
        pin_partner,
        pinned_spins,
        pin_coupling,
        cross_sites,
        cross_coupling,
    ) = refs[:9]
    (
        values,
        dense,
        states,
        high,
        low,
        ahead,
        sent,
        received,
        mixer,
        crosser,
        picker,
        small_sem,
        load_sem,
        value_sem,
        send_sem,
        recv_sem,
    ) = refs[9:]
    wide_log, narrow_log, columns, chunks, kept, bonds, pins = sizes
    rows = PARTS * chunks
    half = columns // 2
    wide, narrow = lax.axis_index("wide"), lax.axis_index("narrow")
    own_bits = (
        bit_at(wide, wide_log - 1),
        bit_at(wide, 0),
        bit_at(narrow, narrow_log - 1),
        bit_at(narrow, 0),
    )

    def flipped(index, bit, position):
        return index + (1 - 2 * bit) * (1 << position)

    partners = (
        (flipped(wide, own_bits[0], wide_log - 1), narrow),
        (flipped(wide, own_bits[1], 0), narrow),
        (wide, flipped(narrow, own_bits[2], narrow_log - 1)),
        (wide, flipped(narrow, own_bits[3], 0)),
    )
    barrier = pltpu.get_barrier_semaphore()
    for partner in partners:
        pl.semaphore_signal(barrier, inc=1, device_id=partner, device_id_type=MESH)

    def load_small(i):
        return pltpu.make_async_copy(smalls[i], refs[i], small_sem.at[i])

    def load(j):
        return pltpu.make_async_copy(
            initial.at[0, 0, :, pl.ds(pl.multiple_of(j * CHUNK, CHUNK), CHUNK)],
            states.at[1, j],
            load_sem.at[j],
        )

    def load_values(j):
        some = pl.ds(PARTS * j, PARTS)
        return pltpu.make_async_copy(
            block_values.at[some], values.at[some, pl.ds(0, kept)], value_sem.at[0]
        )

    def exchange(step, j, k):
        return pltpu.make_async_remote_copy(
            src_ref=sent.at[step, j, k],
            dst_ref=received.at[step, j, k],
            send_sem=send_sem.at[step],
            recv_sem=recv_sem.at[lax.rem(step, 2), j],
            device_id=partners[k],
            device_id_type=MESH,
        )

    def arrival(step, j):
        every = received.at[step, j]
        return pltpu.make_async_copy(every, every, recv_sem.at[lax.rem(step, 2), j])

    def departure(step):
        every = sent.at[step]
        return pltpu.make_async_copy(every, every, send_sem.at[step])

    def store(out, j, state):
        out[0, 0, :, pl.ds(pl.multiple_of(j * CHUNK, CHUNK), CHUNK)] = state

    def keep(step, j, state):
        rounded = state.astype(jnp.bfloat16)
        rest = (state - rounded.astype(jnp.float32)).astype(jnp.bfloat16)
        packed = jnp.dot(picker[...], rounded, preferred_element_type=jnp.float32)
        packed = packed.astype(jnp.bfloat16)
        for h in range(PARTS):
            lanes_of = slice(h * 128, h * 128 + 128)
            high[step, PARTS * j + h] = rounded[:, lanes_of]
            low[step, PARTS * j + h] = rest[:, lanes_of]
            for k in range(CROSS):
                sent[step, j, k, h] = packed[k * half : k * half + half, lanes_of]

    def send(step, j):
        for k in range(CROSS):
            exchange(step, j, k).start()

    load_small(7).start()
    for j in range(chunks):
        load(j).start()
    others = [i for i in range(9) if i != 7]
    for i in others:
        load_small(i).start()
    for j in range(chunks):
        load_values(j).start()
    load_small(7).wait()

    sites = [cross_sites[k] for k in range(CROSS)]
    column = lanes(columns)
    for k in range(CROSS):
        places = jnp.where(
            bit_at(column, sites[k]) == own_bits[k], -1, squeezed(column, sites[k])
        )
        chosen = rows_of(half, columns) == places
        picker[k * half : k * half + half, :] = jnp.where(chosen, 1.0, 0.0).astype(jnp.bfloat16)

    pl.semaphore_wait(barrier, CROSS)

    @pl.loop(0, chunks)
    def _(j):
        load(j).wait()
        keep(0, j, states[1, j])
        send(0, j)

    for i in others:
        load_small(i).wait()
    crossing = [[], []]
    for pair in range(CROSS // 2):
        upper = lanes(columns) >= half
        one, two = 2 * pair, 2 * pair + 1

        def either(first, second):
            return jnp.where(upper, second, first)

        arriving = spread(
            jnp.bitwise_and(lanes(columns), half - 1),
            either(sites[one], sites[two]),
            either(1 - own_bits[one], 1 - own_bits[two]),
        )
        met = rows_of(columns, columns) == arriving
        strengths = zip(split(cross_coupling[one] * 0.5), split(cross_coupling[two] * 0.5))
        for part, (first, second) in zip(crossing, strengths):
            part.append(jnp.where(met, either(first, second), 0.0).astype(jnp.bfloat16))
    for i in range(2):
        crosser[i * columns : i * columns + columns, :] = jnp.concatenate(crossing[i], axis=1)

    row = rows_of(columns, columns)
    hopping = jnp.zeros((columns, columns), jnp.float32)
    diagonal = jnp.zeros((1, columns), jnp.float32)
    for b in range(bonds):
        one, two = bond_sites[0, b], bond_sites[1, b]
        differ = jnp.bitwise_xor(bit_at(column, one), bit_at(column, two)).astype(jnp.float32)
        source = jnp.bitwise_xor(column, jnp.left_shift(1, one) ^ jnp.left_shift(1, two))
        hopping += jnp.where(row == source, bond_coupling[b] * 0.5 * differ, 0.0)
        diagonal += bond_coupling[b] * 0.25 * (1.0 - 2.0 * differ)
    for p in range(pins):
        aligned = jnp.bitwise_xor(bit_at(column, pin_sites[p]), pinned_spins[pin_partner[p]])
        diagonal += pin_coupling[p] * 0.25 * (1.0 - 2.0 * aligned.astype(jnp.float32))
    for k in range(CROSS):
        parity = jnp.bitwise_xor(bit_at(column, sites[k]), own_bits[k])
        diagonal += cross_coupling[k] * 0.25 * (1.0 - 2.0 * parity.astype(jnp.float32))
    matrix = [
        part.astype(jnp.bfloat16) for part in split(hopping + jnp.where(row == column, diagonal, 0.0))
    ]
    mixer[...] = jnp.concatenate([matrix[0], matrix[0], matrix[1]], axis=1)
    states[0] = jnp.zeros(states.shape[1:], jnp.float32)
    values[:, kept] = jnp.zeros((rows, 128, 128), jnp.bfloat16)

    every = values.at[:, pl.ds(0, kept)]
    pltpu.make_async_copy(every, every, value_sem.at[0]).wait()

    @pl.loop(0, chunks)
    def _(j):
        for part in range(PARTS):
            r = PARTS * j + part
            empty = sum(kept << 4 * i for i in range(8))
            places = [jnp.int32(empty - (1 << 32) if empty >> 31 else empty)] * 2
            for q in range(kept):
                wanted = block_index[r, q]
                shift = 4 * jnp.bitwise_and(wanted, 7)
                moved = jnp.left_shift(jnp.int32(q - kept), shift)
                upper = wanted >= 8
                places = [
                    places[0] + jnp.where(upper, 0, moved),
                    places[1] + jnp.where(upper, moved, 0),
                ]
            for m in range(rows):
                q = jnp.bitwise_and(jnp.right_shift(places[m // 8], 4 * (m % 8)), 15)
                dense[j, part, m] = values[r, jnp.minimum(q, kept)]

    def own_product(step, j, first, count, column):
        left = [high[step, first + m] for m in range(count)]
        if column:
            left.append(mixer[...])
        right = []
        for h in range(PARTS):
            blocks = [dense[j, h, first : first + count].reshape(count * 128, 128)]
            if column:
                own_high, own_low = high[step, PARTS * j + h], low[step, PARTS * j + h]
                blocks += [own_high, own_low, own_high]
            right.append(jnp.concatenate(blocks, axis=0))
        return jnp.dot(
            jnp.concatenate(left, axis=1),
            jnp.concatenate(right, axis=1),
            preferred_element_type=jnp.float32,
        )

    def crossing_product(step, j):
        arrived = jnp.concatenate(
            [received[step, j, :, h].reshape(CROSS * half, 128) for h in range(PARTS)], axis=1
        )
        both = jnp.dot(crosser[...], arrived, preferred_element_type=jnp.float32)
        return both[:columns] + both[columns:]

    def arrive(step, j):
        arrival(step, j).wait()

    def next_state(step, j, scale):
        return scale * (ahead[...] + crossing_product(step, j)) - states[step, j]

    ahead[...] = own_product(0, 0, 0, rows, True)

    @pl.loop(0, STEPS - 1)
    def _(step):
        scale = jnp.where(step == 0, 1.0, 2.0)

        def advance(j):
            arrive(step, j)
            state = next_state(step, j, scale)
            states[step + 2, j] = state
            keep(step + 1, j, state)

        @pl.loop(0, chunks - 1)
        def _(j):
            advance(j)
            ahead[...] = own_product(step, j + 1, 0, EARLY, True)
            send(step + 1, j)
            ahead[...] += own_product(step, j + 1, EARLY, rows - EARLY, False)

        advance(chunks - 1)
        ahead[...] = own_product(step + 1, 0, 0, rows - PARTS, True)
        send(step + 1, chunks - 1)
        ahead[...] += own_product(step + 1, 0, rows - PARTS, PARTS, False)

    last = STEPS - 1
    for step in range(last):
        departure(step).wait()

    @pl.loop(0, chunks - 1)
    def _(j):
        store(previous_out, j, states[STEPS, j])
        arrive(last, j)
        store(current_out, j, next_state(last, j, 2.0))
        ahead[...] = own_product(last, j + 1, 0, rows, True)

    store(previous_out, chunks - 1, states[STEPS, chunks - 1])
    departure(last).wait()
    arrive(last, chunks - 1)
    store(current_out, chunks - 1, next_state(last, chunks - 1, 2.0))


def leave(previous, current, previous_out, current_out, sem):
    copies = [
        pltpu.make_async_copy(previous, previous_out, sem.at[0]),
        pltpu.make_async_copy(current, current_out, sem.at[1]),
    ]
    for copy in copies:
        copy.start()
    for copy in copies:
        copy.wait()


def solution(mesh):
    wide_log = mesh.shape["wide"].bit_length() - 1
    narrow_log = mesh.shape["narrow"].bit_length() - 1

    def shards(initial, block_values, block_index, bond_sites, *rest):
        columns, width = initial.shape[2:]
        rows, kept = block_index.shape
        chunks = width // CHUNK
        sizes = (
            wide_log,
            narrow_log,
            columns,
            chunks,
            kept,
            bond_sites.shape[0],
            rest[1].shape[0],
        )
        whole = jax.ShapeDtypeStruct(initial.shape, jnp.float32)
        half_rows = CROSS * columns // 2
        smalls = (block_index, bond_sites.T, *rest)
        parts = pl.pallas_call(
            functools.partial(kernel, sizes),
            out_shape=(whole, whole),
            in_specs=[pl.BlockSpec(memory_space=pltpu.HBM)] * (2 + len(smalls)),
            out_specs=(pl.BlockSpec(memory_space=pltpu.VMEM),) * 2,
            scratch_shapes=[pltpu.SMEM(small.shape, small.dtype) for small in smalls]
            + [
                pltpu.VMEM((rows, kept + 1, 128, 128), jnp.bfloat16),
                pltpu.VMEM((chunks, PARTS, rows, 128, 128), jnp.bfloat16),
                pltpu.VMEM((STEPS + 1, chunks, columns, CHUNK), jnp.float32),
                pltpu.VMEM((STEPS, rows, columns, 128), jnp.bfloat16),
                pltpu.VMEM((STEPS, rows, columns, 128), jnp.bfloat16),
                pltpu.VMEM((columns, CHUNK), jnp.float32),
                pltpu.VMEM((STEPS, chunks, CROSS, PARTS, columns // 2, 128), jnp.bfloat16),
                pltpu.VMEM((STEPS, chunks, CROSS, PARTS, columns // 2, 128), jnp.bfloat16),
                pltpu.VMEM((columns, 3 * columns), jnp.bfloat16),
                pltpu.VMEM((2 * columns, half_rows), jnp.bfloat16),
                pltpu.VMEM((half_rows, columns), jnp.bfloat16),
                pltpu.SemaphoreType.DMA((len(smalls),)),
                pltpu.SemaphoreType.DMA((chunks,)),
                pltpu.SemaphoreType.DMA((1,)),
                pltpu.SemaphoreType.DMA((STEPS,)),
                pltpu.SemaphoreType.DMA((2, chunks)),
            ],
            compiler_params=pltpu.CompilerParams(
                collective_id=0, has_side_effects=True, vmem_limit_bytes=48 * 1024 * 1024
            ),
        )(*[pltpu.with_memory_space_constraint(a, pltpu.HBM) for a in (initial, block_values, *smalls)])
        return pl.pallas_call(
            leave,
            out_shape=(whole, whole),
            in_specs=[pl.BlockSpec(memory_space=pl.ANY)] * 2,
            out_specs=(pl.BlockSpec(memory_space=pltpu.HBM),) * 2,
            scratch_shapes=[pltpu.SemaphoreType.DMA((2,))],
            compiler_params=pltpu.CompilerParams(vmem_limit_bytes=1024 * 1024),
        )(*parts)

    slab = P("wide", "narrow", None, None)
    return jax.shard_map(
        shards,
        mesh=mesh,
        in_specs=(slab,) + (P(),) * 10,
        out_specs=(slab, slab),
        check_vma=False,
    )
```
